32 devices in a mesh: groups: 2 (over x), seq: 8 (over z, y), chan: 2 (over core).
Axes of the slice: x: 2, y: 2, z: 4, core: 2. Of those that a mesh axis runs over, the one named last changes fastest.
Arguments:
- query_proj: bfloat16 [16384, 256], P(('groups', 'seq'), 'chan'), parts along dimension 0, may hold values from -6 to 6
- key_proj: bfloat16 [16384, 256], P(('groups', 'seq'), 'chan'), parts along dimension 0, may hold values from -6 to 6
- value_proj: bfloat16 [16384, 256], P(('groups', 'seq'), 'chan'), parts along dimension 0, may hold values from -6 to 6
- long_filter: float32 [8192, 256], P('seq', 'chan'), may hold values from -4 to 4
- skip_bias: float32 [256], P('chan'), may hold values from -4 to 4
Outputs:
- gated_out: bfloat16 [16384, 256], P(('groups', 'seq'), 'chan'), parts along dimension 0
The draws below stay inside these ranges and needn't reach their ends.
There are 2 independent parts, one for each index of `groups`. The reference program is written for one: setup_inputs(seed, part) draws one part's arguments, and reference() takes and returns one part's arrays. A program takes and returns all parts, laid end to end along the dimension named above; an argument that names none is the same for every part. Nothing has to cross between parts.
All inputs are finite; a program needn't handle non-finite values.
Results may differ from the reference program's by a relative error of at most 0.001.
Values sent between devices are 32-bit elements; how exact they have to be, the bound alone decides.
A program may use at most 64 MiB of HBM per device.

```python
import jax
import jax.numpy as jnp

CHAN = 256
SEQ = 8192


def envelope_energy(lifetimes):
    return jnp.expm1(-2.0 * SEQ / lifetimes) / jnp.expm1(-2.0 / lifetimes)


def draw_long_filter(key, part):
    key_rate = jax.random.fold_in(key, 11)
    key_noise = jax.random.fold_in(key, 12)
    key_slow = jax.random.fold_in(key, 13)
    key_share = jax.random.fold_in(key, 14)
    positions = jnp.arange(SEQ, dtype=jnp.float32)[:, None]
    lifetimes = jnp.exp(jax.random.uniform(key_rate, (CHAN,), jnp.float32, jnp.log(32.0), jnp.log(4.0 * SEQ)))
    noise_vals = jax.random.truncated_normal(key_noise, -4.0, 4.0, (SEQ, CHAN), jnp.float32)
    slow_share = jax.random.uniform(key_share, (CHAN,), jnp.float32, 0.1, 0.3)
    slow_life = jnp.exp(jax.random.uniform(key_slow, (CHAN,), jnp.float32, jnp.log(SEQ / 2.0), jnp.log(4.0 * SEQ)))
    fast_part = jnp.exp(-positions / lifetimes[None, :]) * jnp.sqrt((1.0 - slow_share) / envelope_energy(lifetimes))[None, :]
    slow_part = jnp.exp(-positions / slow_life[None, :]) * jnp.sqrt(slow_share / envelope_energy(slow_life))[None, :]
    return (noise_vals * (fast_part + slow_part)).astype(jnp.float32)


def steps_of(own_key, dims, cuts, smallest, top_value):
    factor_of = 1.0
    for dim, parts in cuts:
        steps = jax.random.uniform(jax.random.fold_in(jax.random.fold_in(own_key, 6), dim), (parts,), jnp.float32, smallest / len(cuts), top_value / len(cuts))
        factor_of = factor_of * jnp.repeat(jnp.exp(steps), dims[dim] // parts).reshape((-1,) + (1,) * (len(dims) - 1 - dim))
    return factor_of


def noise(key, extent, width, most, pieces=(), kind=jnp.bfloat16):
    array = width * jax.random.normal(key, extent, jnp.float32)
    if pieces:
        array = array * steps_of(key, extent, pieces, -0.22, 0.18)
    return jnp.clip(array, -most, most).astype(kind)


def setup_inputs(seed: int = 0, part: int = 0) -> dict:
    streams_of = jax.random.split(jax.random.key(seed), 6)
    own_keys = jax.random.split(jax.random.fold_in(streams_of[5], part), 6)
    query_proj = noise(own_keys[0], (SEQ, CHAN), 1.0, 6.0, ((0, 8), (1, 2)))
    key_proj = noise(own_keys[1], (SEQ, CHAN), 1.0, 6.0, ((0, 8), (1, 2)))
    value_proj = noise(own_keys[2], (SEQ, CHAN), 1.0, 6.0, ((0, 8), (1, 2)))
    long_filter = draw_long_filter(jax.random.fold_in(streams_of[5], 71), part)
    skip_bias = noise(streams_of[4], (CHAN,), 1.0, 4.0, ((0, 2),), jnp.float32)
    return {"query_proj": query_proj, "key_proj": key_proj, "value_proj": value_proj, "long_filter": long_filter, "skip_bias": skip_bias}


def reference(query_proj, key_proj, value_proj, long_filter, skip_bias):
    driver = key_proj.astype(jnp.float32) * value_proj.astype(jnp.float32)
    seq_len = driver.shape[0]
    padded_len = 2 * seq_len
    spectrum = jnp.fft.rfft(driver, n=padded_len, axis=0) * jnp.fft.rfft(long_filter, n=padded_len, axis=0)
    convolved = jnp.fft.irfft(spectrum, n=padded_len, axis=0)[:seq_len]
    gated = query_proj.astype(jnp.float32) * (convolved + skip_bias[None, :] * driver)
    return gated.astype(jnp.bfloat16)
```

```python
import functools
import math

import jax
import jax.numpy as jnp
import numpy as np
from jax import lax
from jax.experimental import pallas as pl
from jax.experimental.pallas import tpu as pltpu
from jax.sharding import PartitionSpec as P

LANES = 128
SUB = 8
UNROLL = 8
MESH = pl.DeviceIdType.MESH
F32 = jnp.float32
BF16 = jnp.bfloat16


def halves(table):
    high = table.astype(BF16)
    low = (table - high.astype(np.float64)).astype(BF16)
    return high, low


def tables(rows):
    length = rows * LANES
    quarter = np.arange(rows) + 0.25
    angle_a = 2.0 * math.pi / rows * np.outer(quarter, np.arange(rows))
    first = np.concatenate((np.cos(angle_a), -np.sin(angle_a)), axis=0)
    last = np.concatenate((np.cos(angle_a.T), -np.sin(angle_a.T)), axis=1) / length
    angle_t = 2.0 * math.pi / length * np.outer(quarter, np.arange(LANES))
    twist = np.stack((np.cos(angle_t), np.sin(angle_t))).astype(np.float32)
    angle_b = 2.0 * math.pi / LANES * (np.outer(np.arange(LANES), np.arange(LANES)) % LANES)
    cosine, sine = np.cos(angle_b), np.sin(angle_b)
    ahead = np.block([[cosine, -sine], [sine, cosine]])
    back = np.block([[cosine, sine], [-sine, cosine]])
    first_hi, first_lo = halves(first)
    last_hi, last_lo = halves(last)
    return (
        np.concatenate((first_hi, first_hi, first_lo), axis=1),
        np.concatenate((last_hi, last_hi, last_lo), axis=1),
        twist,
        np.stack(halves(ahead)),
        np.stack(halves(back)),
    )


def split(value):
    high = value.astype(BF16)
    return high, (value - high.astype(F32)).astype(BF16)


def dot(left, right):
    return jnp.dot(left, right, preferred_element_type=F32)


def times_table(value, table_ref):
    high, low = split(value)
    return dot(high, table_ref[0]) + dot(low, table_ref[0]) + dot(high, table_ref[1])


def table_times(table3, value):
    high, low = split(value)
    return dot(table3, jnp.concatenate((high, low, high), axis=0))


def body(n, groups, share, step, *refs):
    inputs, out_ref = refs[:10], refs[10]
    held = refs[11:21]
    (out_u, out_h, in_u, in_h, out_y, in_y, spec_h,
     send_sem, recv_u_sem, recv_h_sem, recv_sem, own_sem, load_sem) = refs[21:]
    loads = [pltpu.make_async_copy(inputs[i], held[i], load_sem.at[i]) for i in range(10)]
    for i in (3, 1, 2, 5, 7, 8, 9, 6, 0, 4):
        loads[i].start()
    (q_ref, k_ref, v_ref, h_ref, skip_ref,
     first_ref, last_ref, twist_ref, ahead_ref, back_ref) = held
    me = lax.axis_index("seq")
    group = lax.axis_index("groups")
    part = share // groups
    blocks = k_ref.shape[0] // LANES
    rows = n * blocks
    chunks = share // step

    def wrap(i, size):
        return jnp.where(i >= size, i - size, i)

    def peer_of(i):
        return wrap(me + i, n)

    def each_peer(act):
        if n <= UNROLL:
            for i in range(1, n):
                act(peer_of(i))
            return

        def go(i, carry):
            act(peer_of(i))
            return carry

        lax.fori_loop(1, n, go, 0)

    def drain(ref, height, sem):
        where = ref.at[pl.ds(0, height)]
        pltpu.make_async_copy(where, where, sem).wait()

    barrier = pltpu.get_barrier_semaphore()

    each_peer(lambda p: pl.semaphore_signal(
        barrier, inc=1, device_id={"seq": p}, device_id_type=MESH))
    for other in range(1, groups):
        pl.semaphore_signal(barrier, inc=1, device_id={"groups": wrap(group + other, groups)},
                            device_id_type=MESH)

    loads[3].wait()
    for a in range(blocks):
        tile = h_ref[pl.ds(a * LANES, LANES), :]
        out_h[pl.ds(a, LANES, stride=blocks), :] = tile.T
    pl.semaphore_wait(barrier, n + groups - 2)

    def slab(owner, j, width):
        return pl.ds(pl.multiple_of((owner * share + j * width) * blocks, SUB), width * blocks)

    def piece(owner, which):
        return pl.ds(pl.multiple_of((owner * share + which * part) * blocks, SUB), part * blocks)

    def h_copy(owner, sender, peer):
        return pltpu.make_async_remote_copy(
            src_ref=out_h.at[piece(owner, group)],
            dst_ref=in_h.at[sender, piece(0, group)],
            send_sem=send_sem.at[0],
            recv_sem=recv_h_sem.at[sender],
            device_id={"seq": peer},
            device_id_type=MESH,
        )

    def h_pass(other, which, sender):
        return pltpu.make_async_remote_copy(
            src_ref=in_h.at[sender, piece(0, which)],
            dst_ref=in_h.at[sender, piece(0, which)],
            send_sem=send_sem.at[1],
            recv_sem=recv_sem.at[0],
            device_id={"groups": wrap(group + other, groups)},
            device_id_type=MESH,
        )

    def u_copy(j, owner, sender, peer):
        return pltpu.make_async_remote_copy(
            src_ref=out_u.at[slab(owner, j, step)],
            dst_ref=in_u.at[sender, slab(0, j, step)],
            send_sem=send_sem.at[2],
            recv_sem=recv_u_sem.at[j],
            device_id={"seq": peer},
            device_id_type=MESH,
        )

    def y_copy(j, owner, sender, peer):
        return pltpu.make_async_remote_copy(
            src_ref=out_y.at[owner, slab(0, j, step)],
            dst_ref=in_y.at[slab(sender, j, step)],
            send_sem=send_sem.at[3],
            recv_sem=recv_sem.at[1],
            device_id={"seq": peer},
            device_id_type=MESH,
        )

    each_peer(lambda p: h_copy(p, me, p).start())
    own_h = pltpu.make_async_copy(
        out_h.at[slab(me, 0, share)], in_h.at[me], own_sem.at[0])
    own_h.start()

    loads[1].wait()
    loads[2].wait()
    for a in range(blocks):
        where = pl.ds(a * LANES, LANES)
        tile = k_ref[where, :].astype(F32) * v_ref[where, :].astype(F32)
        out_u[pl.ds(a, LANES, stride=blocks), :] = tile.T
    for j in range(chunks):
        each_peer(lambda p: u_copy(j, p, me, p).start())
    own_u = pltpu.make_async_copy(out_u.at[slab(me, 0, share)], in_u.at[me], own_sem.at[1])
    own_u.start()

    def forward(ref, j):
        parts = []
        for pair in range(0, step, 2):
            both = []
            for c in (pair, pair + 1):
                at = pl.ds(pl.multiple_of((j * step + c) * blocks, SUB), blocks)
                both.append(ref[:, at, :].reshape(rows, LANES))
            mixed = table_times(first_ref[...], jnp.concatenate(both, axis=1))
            for c in range(2):
                real = mixed[:rows, c * LANES:(c + 1) * LANES]
                imag = mixed[rows:, c * LANES:(c + 1) * LANES]
                cosine, sine = twist_ref[0], twist_ref[1]
                parts.append(jnp.concatenate(
                    (real * cosine + imag * sine, imag * cosine - real * sine), axis=1))
        return times_table(jnp.concatenate(parts, axis=0), ahead_ref)

    def pass_on(sender):
        for other in range(1, groups):
            h_pass(other, group, sender).start()

    def hand_on(sender):
        h_copy(me, sender, sender).wait_recv()
        pass_on(sender)

    each_peer(hand_on)
    own_h.wait()
    for i in (5, 7, 8):
        loads[i].wait()

    drain(out_h, (groups - 1) * (n - 1) * part * blocks, recv_sem.at[0])

    def filter_step(j, carry):
        spec_h[j] = forward(in_h, j)
        return carry

    lax.fori_loop(0, chunks, filter_step, 0)
    own_u.wait()
    loads[6].wait()
    loads[9].wait()

    def chunk_step(j, carry):
        arrived = in_u.at[pl.ds(0, n - 1), slab(0, j, step)]
        pltpu.make_async_copy(arrived, arrived, recv_u_sem.at[j]).wait()
        spec = forward(in_u, j)
        other = spec_h[j]
        ur, ui = spec[:, :LANES], spec[:, LANES:]
        hr, hi = other[:, :LANES], other[:, LANES:]
        prod = jnp.concatenate((ur * hr - ui * hi, ur * hi + ui * hr), axis=1)
        turned = times_table(prod, back_ref)
        for pair in range(0, step, 2):
            both = []
            for c in (pair, pair + 1):
                real = turned[c * rows:(c + 1) * rows, :LANES]
                imag = turned[c * rows:(c + 1) * rows, LANES:]
                cosine, sine = twist_ref[0], twist_ref[1]
                both.append(jnp.concatenate(
                    (real * cosine - imag * sine, real * sine + imag * cosine), axis=0))
            result = table_times(last_ref[...], jnp.concatenate(both, axis=1))
            for c in range(2):
                at = pl.ds(pl.multiple_of((j * step + pair + c) * blocks, SUB), blocks)
                out_y[:, at, :] = result[:, c * LANES:(c + 1) * LANES].reshape(n, blocks, LANES)
        each_peer(lambda p: y_copy(j, p, me, p).start())
        return carry

    lax.fori_loop(0, chunks, chunk_step, 0)
    own_y = pltpu.make_async_copy(out_y.at[me], in_y.at[slab(me, 0, share)], own_sem.at[2])
    own_y.start()
    own_y.wait()
    loads[0].wait()
    loads[4].wait()
    drain(out_h, (n - 1) * part * blocks, send_sem.at[0])
    drain(out_h, (groups - 1) * (n - 1) * part * blocks, send_sem.at[1])
    drain(out_u, (n - 1) * share * blocks, send_sem.at[2])
    drain(in_y, (n - 1) * share * blocks, recv_sem.at[1])

    for a in range(blocks):
        where = pl.ds(a * LANES, LANES)
        driver = k_ref[where, :].astype(F32) * v_ref[where, :].astype(F32)
        conv = in_y[pl.ds(a, LANES, stride=blocks), :].T
        out_ref[where, :] = (
            q_ref[where, :].astype(F32) * (conv + skip_ref[...] * driver)
        ).astype(BF16)

    drain(in_y, (n - 1) * share * blocks, send_sem.at[3])


def shards(n, groups, query_proj, key_proj, value_proj, long_filter, skip_bias):
    tokens, chans = key_proj.shape
    share = chans // n
    step = min(8, share)
    chunks = share // step
    blocks = tokens // LANES
    rows = n * blocks
    operands = (
        query_proj, key_proj, value_proj, long_filter, skip_bias.reshape(1, chans), *tables(rows))
    return pl.pallas_call(
        functools.partial(body, n, groups, share, step),
        out_shape=jax.ShapeDtypeStruct((tokens, chans), BF16),
        in_specs=[pl.BlockSpec(memory_space=pltpu.HBM)] * len(operands),
        out_specs=pl.BlockSpec(memory_space=pltpu.VMEM),
        scratch_shapes=[pltpu.VMEM(x.shape, x.dtype) for x in operands] + [
            pltpu.VMEM((chans * blocks, LANES), F32),
            pltpu.VMEM((chans * blocks, LANES), F32),
            pltpu.VMEM((n, share * blocks, LANES), F32),
            pltpu.VMEM((n, share * blocks, LANES), F32),
            pltpu.VMEM((n, share * blocks, LANES), F32),
            pltpu.VMEM((chans * blocks, LANES), F32),
            pltpu.VMEM((chunks, step * rows, 2 * LANES), F32),
            pltpu.SemaphoreType.DMA((4,)),
            pltpu.SemaphoreType.DMA((chunks,)),
            pltpu.SemaphoreType.DMA((n,)),
            pltpu.SemaphoreType.DMA((2,)),
            pltpu.SemaphoreType.DMA((3,)),
            pltpu.SemaphoreType.DMA((len(operands),)),
        ],
        compiler_params=pltpu.CompilerParams(
            collective_id=0, has_side_effects=True, vmem_limit_bytes=48 * 1024 * 1024
        ),
        name="hyena_conv",
    )(*[pltpu.with_memory_space_constraint(x, pltpu.HBM) for x in operands])


def solution(mesh):
    placed = (
        P(("groups", "seq"), "chan"),
        P(("groups", "seq"), "chan"),
        P(("groups", "seq"), "chan"),
        P("seq", "chan"),
        P("chan"),
    )
    return jax.shard_map(
        functools.partial(shards, mesh.shape["seq"], mesh.shape["groups"]),
        mesh=mesh,
        in_specs=placed,
        out_specs=P(("groups", "seq"), "chan"),
        check_vma=False,
    )
```

```python
import functools
import math

import jax
import jax.numpy as jnp
import numpy as np
from jax import lax
from jax.experimental import pallas as pl
from jax.experimental.pallas import tpu as pltpu
from jax.sharding import PartitionSpec as P

LANES = 128
SUB = 8
UNROLL = 8
MESH = pl.DeviceIdType.MESH
F32 = jnp.float32
BF16 = jnp.bfloat16


def halves(table):
    high = table.astype(BF16)
    low = (table - high.astype(np.float64)).astype(BF16)
    return high, low


def tables(rows):
    length = rows * LANES
    quarter = np.arange(rows) + 0.25
    angle_a = 2.0 * math.pi / rows * np.outer(quarter, np.arange(rows))
    first = np.concatenate((np.cos(angle_a), -np.sin(angle_a)), axis=0)
    last = np.concatenate((np.cos(angle_a.T), -np.sin(angle_a.T)), axis=1) / length
    angle_t = 2.0 * math.pi / length * np.outer(quarter, np.arange(LANES))
    twist = np.stack((np.cos(angle_t), np.sin(angle_t))).astype(np.float32)
    angle_b = 2.0 * math.pi / LANES * (np.outer(np.arange(LANES), np.arange(LANES)) % LANES)
    cosine, sine = np.cos(angle_b), np.sin(angle_b)
    ahead = np.block([[cosine, -sine], [sine, cosine]])
    back = np.block([[cosine, sine], [-sine, cosine]])
    first_hi, first_lo = halves(first)
    last_hi, last_lo = halves(last)
    return (
        np.concatenate((first_hi, first_hi, first_lo), axis=1),
        np.concatenate((last_hi, last_hi, last_lo), axis=1),
        twist,
        np.stack(halves(ahead)),
        np.stack(halves(back)),
    )


def split(value):
    high = value.astype(BF16)
    return high, (value - high.astype(F32)).astype(BF16)


def dot(left, right):
    return jnp.dot(left, right, preferred_element_type=F32)


def times_table(value, table_ref):
    high, low = split(value)
    return dot(high, table_ref[0]) + dot(low, table_ref[0]) + dot(high, table_ref[1])


def table_times(table3, value):
    high, low = split(value)
    return dot(table3, jnp.concatenate((high, low, high), axis=0))


def body(n, groups, share, step, *refs):
    inputs, out_ref = refs[:10], refs[10]
    held = refs[11:21]
    (out_u, out_h, in_u, in_h, out_y, in_y, spec_h,
     send_sem, recv_u_sem, recv_h_sem, recv_sem, own_sem, load_sem) = refs[21:]
    loads = [pltpu.make_async_copy(inputs[i], held[i], load_sem.at[i]) for i in range(10)]
    for i in (3, 1, 2, 5, 7, 8, 9, 6, 0, 4):
        loads[i].start()
    (q_ref, k_ref, v_ref, h_ref, skip_ref,
     first_ref, last_ref, twist_ref, ahead_ref, back_ref) = held
    me = lax.axis_index("seq")
    group = lax.axis_index("groups")
    part = share // groups
    blocks = k_ref.shape[0] // LANES
    rows = n * blocks
    chunks = share // step

    def wrap(i, size):
        return jnp.where(i >= size, i - size, i)

    def peer_of(i):
        return wrap(me + i, n)

    def each_peer(act, back=False):
        if n <= UNROLL:
            for i in range(1, n):
                act(peer_of(n - i if back else i))
            return

        def go(i, carry):
            act(peer_of(n - i if back else i))
            return carry

        lax.fori_loop(1, n, go, 0)

    def drain(ref, height, sem):
        where = ref.at[pl.ds(0, height)]
        pltpu.make_async_copy(where, where, sem).wait()

    barrier = pltpu.get_barrier_semaphore()

    each_peer(lambda p: pl.semaphore_signal(
        barrier, inc=1, device_id={"seq": p}, device_id_type=MESH))
    for other in range(1, groups):
        pl.semaphore_signal(barrier, inc=1, device_id={"groups": wrap(group + other, groups)},
                            device_id_type=MESH)

    loads[3].wait()
    for a in range(blocks):
        tile = h_ref[pl.ds(a * LANES, LANES), :]
        out_h[pl.ds(a, LANES, stride=blocks), :] = tile.T
    pl.semaphore_wait(barrier, n + groups - 2)

    def slab(owner, j, width):
        return pl.ds(pl.multiple_of((owner * share + j * width) * blocks, SUB), width * blocks)

    def piece(owner, which):
        return pl.ds(pl.multiple_of((owner * share + which * part) * blocks, SUB), part * blocks)

    def h_copy(owner, sender, peer):
        return pltpu.make_async_remote_copy(
            src_ref=out_h.at[piece(owner, group)],
            dst_ref=in_h.at[sender, piece(0, group)],
            send_sem=send_sem.at[0],
            recv_sem=recv_h_sem.at[sender],
            device_id={"seq": peer},
            device_id_type=MESH,
        )

    def h_pass(other, which, sender):
        return pltpu.make_async_remote_copy(
            src_ref=in_h.at[sender, piece(0, which)],
            dst_ref=in_h.at[sender, piece(0, which)],
            send_sem=send_sem.at[1],
            recv_sem=recv_sem.at[0],
            device_id={"groups": wrap(group + other, groups)},
            device_id_type=MESH,
        )

    def u_copy(j, owner, sender, peer):
        return pltpu.make_async_remote_copy(
            src_ref=out_u.at[slab(owner, j, step)],
            dst_ref=in_u.at[sender, slab(0, j, step)],
            send_sem=send_sem.at[2],
            recv_sem=recv_u_sem.at[j],
            device_id={"seq": peer},
            device_id_type=MESH,
        )

    def y_copy(j, owner, sender, peer):
        return pltpu.make_async_remote_copy(
            src_ref=out_y.at[owner, slab(0, j, step)],
            dst_ref=in_y.at[slab(sender, j, step)],
            send_sem=send_sem.at[3],
            recv_sem=recv_sem.at[1],
            device_id={"seq": peer},
            device_id_type=MESH,
        )

    each_peer(lambda p: h_copy(p, me, p).start())
    own_h = pltpu.make_async_copy(
        out_h.at[slab(me, 0, share)], in_h.at[me], own_sem.at[0])
    own_h.start()

    loads[1].wait()
    loads[2].wait()
    for a in range(blocks):
        where = pl.ds(a * LANES, LANES)
        tile = k_ref[where, :].astype(F32) * v_ref[where, :].astype(F32)
        out_u[pl.ds(a, LANES, stride=blocks), :] = tile.T
    for j in range(chunks):
        each_peer(lambda p: u_copy(j, p, me, p).start(), back=True)
    own_u = pltpu.make_async_copy(out_u.at[slab(me, 0, share)], in_u.at[me], own_sem.at[1])
    own_u.start()

    def forward(ref, j):
        parts = []
        for pair in range(0, step, 2):
            both = []
            for c in (pair, pair + 1):
                at = pl.ds(pl.multiple_of((j * step + c) * blocks, SUB), blocks)
                both.append(ref[:, at, :].reshape(rows, LANES))
            mixed = table_times(first_ref[...], jnp.concatenate(both, axis=1))
            for c in range(2):
                real = mixed[:rows, c * LANES:(c + 1) * LANES]
                imag = mixed[rows:, c * LANES:(c + 1) * LANES]
                cosine, sine = twist_ref[0], twist_ref[1]
                parts.append(jnp.concatenate(
                    (real * cosine + imag * sine, imag * cosine - real * sine), axis=1))
        return times_table(jnp.concatenate(parts, axis=0), ahead_ref)

    def pass_on(sender):
        for other in range(1, groups):
            h_pass(other, group, sender).start()

    def hand_on(sender):
        h_copy(me, sender, sender).wait_recv()
        pass_on(sender)

    each_peer(hand_on)
    own_h.wait()
    for i in (5, 7, 8):
        loads[i].wait()

    drain(out_h, (groups - 1) * (n - 1) * part * blocks, recv_sem.at[0])

    def filter_step(j, carry):
        spec_h[j] = forward(in_h, j)
        return carry

    lax.fori_loop(0, chunks, filter_step, 0)
    own_u.wait()
    loads[6].wait()
    loads[9].wait()

    def chunk_step(j, carry):
        arrived = in_u.at[pl.ds(0, n - 1), slab(0, j, step)]
        pltpu.make_async_copy(arrived, arrived, recv_u_sem.at[j]).wait()
        spec = forward(in_u, j)
        other = spec_h[j]
        ur, ui = spec[:, :LANES], spec[:, LANES:]
        hr, hi = other[:, :LANES], other[:, LANES:]
        prod = jnp.concatenate((ur * hr - ui * hi, ur * hi + ui * hr), axis=1)
        turned = times_table(prod, back_ref)
        for pair in range(0, step, 2):
            both = []
            for c in (pair, pair + 1):
                real = turned[c * rows:(c + 1) * rows, :LANES]
                imag = turned[c * rows:(c + 1) * rows, LANES:]
                cosine, sine = twist_ref[0], twist_ref[1]
                both.append(jnp.concatenate(
                    (real * cosine - imag * sine, real * sine + imag * cosine), axis=0))
            result = table_times(last_ref[...], jnp.concatenate(both, axis=1))
            for c in range(2):
                at = pl.ds(pl.multiple_of((j * step + pair + c) * blocks, SUB), blocks)
                out_y[:, at, :] = result[:, c * LANES:(c + 1) * LANES].reshape(n, blocks, LANES)
        each_peer(lambda p: y_copy(j, p, me, p).start())
        return carry

    lax.fori_loop(0, chunks, chunk_step, 0)
    own_y = pltpu.make_async_copy(out_y.at[me], in_y.at[slab(me, 0, share)], own_sem.at[2])
    own_y.start()
    own_y.wait()
    loads[0].wait()
    loads[4].wait()
    drain(out_h, (n - 1) * part * blocks, send_sem.at[0])
    drain(out_h, (groups - 1) * (n - 1) * part * blocks, send_sem.at[1])
    drain(out_u, (n - 1) * share * blocks, send_sem.at[2])
    drain(in_y, (n - 1) * share * blocks, recv_sem.at[1])

    for a in range(blocks):
        where = pl.ds(a * LANES, LANES)
        driver = k_ref[where, :].astype(F32) * v_ref[where, :].astype(F32)
        conv = in_y[pl.ds(a, LANES, stride=blocks), :].T
        out_ref[where, :] = (
            q_ref[where, :].astype(F32) * (conv + skip_ref[...] * driver)
        ).astype(BF16)

    drain(in_y, (n - 1) * share * blocks, send_sem.at[3])


def shards(n, groups, query_proj, key_proj, value_proj, long_filter, skip_bias):
    tokens, chans = key_proj.shape
    share = chans // n
    step = min(8, share)
    chunks = share // step
    blocks = tokens // LANES
    rows = n * blocks
    operands = (
        query_proj, key_proj, value_proj, long_filter, skip_bias.reshape(1, chans), *tables(rows))
    return pl.pallas_call(
        functools.partial(body, n, groups, share, step),
        out_shape=jax.ShapeDtypeStruct((tokens, chans), BF16),
        in_specs=[pl.BlockSpec(memory_space=pltpu.HBM)] * len(operands),
        out_specs=pl.BlockSpec(memory_space=pltpu.VMEM),
        scratch_shapes=[pltpu.VMEM(x.shape, x.dtype) for x in operands] + [
            pltpu.VMEM((chans * blocks, LANES), F32),
            pltpu.VMEM((chans * blocks, LANES), F32),
            pltpu.VMEM((n, share * blocks, LANES), F32),
            pltpu.VMEM((n, share * blocks, LANES), F32),
            pltpu.VMEM((n, share * blocks, LANES), F32),
            pltpu.VMEM((chans * blocks, LANES), F32),
            pltpu.VMEM((chunks, step * rows, 2 * LANES), F32),
            pltpu.SemaphoreType.DMA((4,)),
            pltpu.SemaphoreType.DMA((chunks,)),
            pltpu.SemaphoreType.DMA((n,)),
            pltpu.SemaphoreType.DMA((2,)),
            pltpu.SemaphoreType.DMA((3,)),
            pltpu.SemaphoreType.DMA((len(operands),)),
        ],
        compiler_params=pltpu.CompilerParams(
            collective_id=0, has_side_effects=True, vmem_limit_bytes=48 * 1024 * 1024
        ),
        name="hyena_conv",
    )(*[pltpu.with_memory_space_constraint(x, pltpu.HBM) for x in operands])


def solution(mesh):
    placed = (
        P(("groups", "seq"), "chan"),
        P(("groups", "seq"), "chan"),
        P(("groups", "seq"), "chan"),
        P("seq", "chan"),
        P("chan"),
    )
    return jax.shard_map(
        functools.partial(shards, mesh.shape["seq"], mesh.shape["groups"]),
        mesh=mesh,
        in_specs=placed,
        out_specs=P(("groups", "seq"), "chan"),
        check_vma=False,
    )
```

```python
import functools
import math

import jax
import jax.numpy as jnp
import numpy as np
from jax import lax
from jax.experimental import pallas as pl
from jax.experimental.pallas import tpu as pltpu
from jax.sharding import PartitionSpec as P

LANES = 128
SUB = 8
UNROLL = 8
MESH = pl.DeviceIdType.MESH
F32 = jnp.float32
BF16 = jnp.bfloat16


def halves(table):
    high = table.astype(BF16)
    low = (table - high.astype(np.float64)).astype(BF16)
    return high, low


def tables(rows):
    length = rows * LANES
    quarter = np.arange(rows) + 0.25
    angle_a = 2.0 * math.pi / rows * np.outer(quarter, np.arange(rows))
    first = np.concatenate((np.cos(angle_a), -np.sin(angle_a)), axis=0)
    last = np.concatenate((np.cos(angle_a.T), -np.sin(angle_a.T)), axis=1) / length
    angle_t = 2.0 * math.pi / length * np.outer(quarter, np.arange(LANES))
    twist = np.stack((np.cos(angle_t), np.sin(angle_t))).astype(np.float32)
    angle_b = 2.0 * math.pi / LANES * (np.outer(np.arange(LANES), np.arange(LANES)) % LANES)
    cosine, sine = np.cos(angle_b), np.sin(angle_b)
    ahead = np.block([[cosine, -sine], [sine, cosine]])
    back = np.block([[cosine, sine], [-sine, cosine]])
    first_hi, first_lo = halves(first)
    last_hi, last_lo = halves(last)
    return (
        np.concatenate((first_hi, first_hi, first_lo), axis=1),
        np.concatenate((last_hi, last_hi, last_lo), axis=1),
        twist,
        np.stack(halves(ahead)),
        np.stack(halves(back)),
    )


def split(value):
    high = value.astype(BF16)
    return high, (value - high.astype(F32)).astype(BF16)


def dot(left, right):
    return jnp.dot(left, right, preferred_element_type=F32)


def times_table(value, table_ref):
    high, low = split(value)
    return dot(high, table_ref[0]) + dot(low, table_ref[0]) + dot(high, table_ref[1])


def table_times(table3, value):
    high, low = split(value)
    return dot(table3, jnp.concatenate((high, low, high), axis=0))


def body(n, groups, share, step, *refs):
    inputs, out_ref = refs[:10], refs[10]
    held = refs[11:21]
    (out_u, out_h, in_u, in_h, out_y, in_y, spec_h,
     send_sem, recv_u_sem, recv_h_sem, recv_sem, own_sem, load_sem) = refs[21:]
    loads = [pltpu.make_async_copy(inputs[i], held[i], load_sem.at[i]) for i in range(10)]
    for i in (3, 1, 2, 5, 7, 8, 9, 6, 0, 4):
        loads[i].start()
    (q_ref, k_ref, v_ref, h_ref, skip_ref,
     first_ref, last_ref, twist_ref, ahead_ref, back_ref) = held
    me = lax.axis_index("seq")
    group = lax.axis_index("groups")
    part = share // groups
    blocks = k_ref.shape[0] // LANES
    rows = n * blocks
    chunks = share // step

    def wrap(i, size):
        return jnp.where(i >= size, i - size, i)

    def peer_of(i):
        return wrap(me + i, n)

    def each_peer(act, back=False):
        if n <= UNROLL:
            for i in range(1, n):
                act(peer_of(n - i if back else i))
            return

        def go(i, carry):
            act(peer_of(n - i if back else i))
            return carry

        lax.fori_loop(1, n, go, 0)

    def drain(ref, height, sem):
        where = ref.at[pl.ds(0, height)]
        pltpu.make_async_copy(where, where, sem).wait()

    barrier = pltpu.get_barrier_semaphore()

    each_peer(lambda p: pl.semaphore_signal(
        barrier, inc=1, device_id={"seq": p}, device_id_type=MESH), back=True)
    for other in range(1, groups):
        pl.semaphore_signal(barrier, inc=1, device_id={"groups": wrap(group + other, groups)},
                            device_id_type=MESH)

    loads[3].wait()
    for a in range(blocks):
        tile = h_ref[pl.ds(a * LANES, LANES), :]
        out_h[pl.ds(a, LANES, stride=blocks), :] = tile.T
    pl.semaphore_wait(barrier, n + groups - 2)

    def slab(owner, j, width):
        return pl.ds(pl.multiple_of((owner * share + j * width) * blocks, SUB), width * blocks)

    def piece(owner, which):
        return pl.ds(pl.multiple_of((owner * share + which * part) * blocks, SUB), part * blocks)

    def h_copy(owner, sender, peer):
        return pltpu.make_async_remote_copy(
            src_ref=out_h.at[piece(owner, group)],
            dst_ref=in_h.at[sender, piece(0, group)],
            send_sem=send_sem.at[0],
            recv_sem=recv_h_sem.at[sender],
            device_id={"seq": peer},
            device_id_type=MESH,
        )

    def h_pass(other, which, sender):
        return pltpu.make_async_remote_copy(
            src_ref=in_h.at[sender, piece(0, which)],
            dst_ref=in_h.at[sender, piece(0, which)],
            send_sem=send_sem.at[1],
            recv_sem=recv_sem.at[0],
            device_id={"groups": wrap(group + other, groups)},
            device_id_type=MESH,
        )

    def u_copy(j, owner, sender, peer):
        return pltpu.make_async_remote_copy(
            src_ref=out_u.at[slab(owner, j, step)],
            dst_ref=in_u.at[sender, slab(0, j, step)],
            send_sem=send_sem.at[2],
            recv_sem=recv_u_sem.at[j],
            device_id={"seq": peer},
            device_id_type=MESH,
        )

    def y_copy(j, owner, sender, peer):
        return pltpu.make_async_remote_copy(
            src_ref=out_y.at[owner, slab(0, j, step)],
            dst_ref=in_y.at[slab(sender, j, step)],
            send_sem=send_sem.at[3],
            recv_sem=recv_sem.at[1],
            device_id={"seq": peer},
            device_id_type=MESH,
        )

    each_peer(lambda p: h_copy(p, me, p).start())
    own_h = pltpu.make_async_copy(
        out_h.at[slab(me, 0, share)], in_h.at[me], own_sem.at[0])
    own_h.start()

    loads[1].wait()
    loads[2].wait()
    for a in range(blocks):
        where = pl.ds(a * LANES, LANES)
        tile = k_ref[where, :].astype(F32) * v_ref[where, :].astype(F32)
        out_u[pl.ds(a, LANES, stride=blocks), :] = tile.T
    for j in range(chunks):
        each_peer(lambda p: u_copy(j, p, me, p).start(), back=True)
    own_u = pltpu.make_async_copy(out_u.at[slab(me, 0, share)], in_u.at[me], own_sem.at[1])
    own_u.start()

    def forward(ref, j):
        parts = []
        for pair in range(0, step, 2):
            both = []
            for c in (pair, pair + 1):
                at = pl.ds(pl.multiple_of((j * step + c) * blocks, SUB), blocks)
                both.append(ref[:, at, :].reshape(rows, LANES))
            mixed = table_times(first_ref[...], jnp.concatenate(both, axis=1))
            for c in range(2):
                real = mixed[:rows, c * LANES:(c + 1) * LANES]
                imag = mixed[rows:, c * LANES:(c + 1) * LANES]
                cosine, sine = twist_ref[0], twist_ref[1]
                parts.append(jnp.concatenate(
                    (real * cosine + imag * sine, imag * cosine - real * sine), axis=1))
        return times_table(jnp.concatenate(parts, axis=0), ahead_ref)

    def pass_on(sender):
        for other in range(1, groups):
            h_pass(other, group, sender).start()

    def hand_on(sender):
        h_copy(me, sender, sender).wait_recv()
        pass_on(sender)

    each_peer(hand_on)
    own_h.wait()
    for i in (5, 7, 8):
        loads[i].wait()

    drain(out_h, (groups - 1) * (n - 1) * part * blocks, recv_sem.at[0])

    def filter_step(j, carry):
        spec_h[j] = forward(in_h, j)
        return carry

    lax.fori_loop(0, chunks, filter_step, 0)
    own_u.wait()
    loads[6].wait()
    loads[9].wait()

    def chunk_step(j, carry):
        arrived = in_u.at[pl.ds(0, n - 1), slab(0, j, step)]
        pltpu.make_async_copy(arrived, arrived, recv_u_sem.at[j]).wait()
        spec = forward(in_u, j)
        other = spec_h[j]
        ur, ui = spec[:, :LANES], spec[:, LANES:]
        hr, hi = other[:, :LANES], other[:, LANES:]
        prod = jnp.concatenate((ur * hr - ui * hi, ur * hi + ui * hr), axis=1)
        turned = times_table(prod, back_ref)
        for pair in range(0, step, 2):
            both = []
            for c in (pair, pair + 1):
                real = turned[c * rows:(c + 1) * rows, :LANES]
                imag = turned[c * rows:(c + 1) * rows, LANES:]
                cosine, sine = twist_ref[0], twist_ref[1]
                both.append(jnp.concatenate(
                    (real * cosine - imag * sine, real * sine + imag * cosine), axis=0))
            result = table_times(last_ref[...], jnp.concatenate(both, axis=1))
            for c in range(2):
                at = pl.ds(pl.multiple_of((j * step + pair + c) * blocks, SUB), blocks)
                out_y[:, at, :] = result[:, c * LANES:(c + 1) * LANES].reshape(n, blocks, LANES)
        each_peer(lambda p: y_copy(j, p, me, p).start())
        return carry

    lax.fori_loop(0, chunks, chunk_step, 0)
    own_y = pltpu.make_async_copy(out_y.at[me], in_y.at[slab(me, 0, share)], own_sem.at[2])
    own_y.start()
    loads[0].wait()
    loads[4].wait()
    drain(out_h, (n - 1) * part * blocks, send_sem.at[0])
    drain(out_h, (groups - 1) * (n - 1) * part * blocks, send_sem.at[1])
    drain(out_u, (n - 1) * share * blocks, send_sem.at[2])
    drain(in_y, (n - 1) * share * blocks, recv_sem.at[1])
    own_y.wait()

    for a in range(blocks):
        where = pl.ds(a * LANES, LANES)
        driver = k_ref[where, :].astype(F32) * v_ref[where, :].astype(F32)
        conv = in_y[pl.ds(a, LANES, stride=blocks), :].T
        out_ref[where, :] = (
            q_ref[where, :].astype(F32) * (conv + skip_ref[...] * driver)
        ).astype(BF16)

    drain(in_y, (n - 1) * share * blocks, send_sem.at[3])


def shards(n, groups, query_proj, key_proj, value_proj, long_filter, skip_bias):
    tokens, chans = key_proj.shape
    share = chans // n
    step = min(8, share)
    chunks = share // step
    blocks = tokens // LANES
    rows = n * blocks
    operands = (
        query_proj, key_proj, value_proj, long_filter, skip_bias.reshape(1, chans), *tables(rows))
    return pl.pallas_call(
        functools.partial(body, n, groups, share, step),
        out_shape=jax.ShapeDtypeStruct((tokens, chans), BF16),
        in_specs=[pl.BlockSpec(memory_space=pltpu.HBM)] * len(operands),
        out_specs=pl.BlockSpec(memory_space=pltpu.VMEM),
        scratch_shapes=[pltpu.VMEM(x.shape, x.dtype) for x in operands] + [
            pltpu.VMEM((chans * blocks, LANES), F32),
            pltpu.VMEM((chans * blocks, LANES), F32),
            pltpu.VMEM((n, share * blocks, LANES), F32),
            pltpu.VMEM((n, share * blocks, LANES), F32),
            pltpu.VMEM((n, share * blocks, LANES), F32),
            pltpu.VMEM((chans * blocks, LANES), F32),
            pltpu.VMEM((chunks, step * rows, 2 * LANES), F32),
            pltpu.SemaphoreType.DMA((4,)),
            pltpu.SemaphoreType.DMA((chunks,)),
            pltpu.SemaphoreType.DMA((n,)),
            pltpu.SemaphoreType.DMA((2,)),
            pltpu.SemaphoreType.DMA((3,)),
            pltpu.SemaphoreType.DMA((len(operands),)),
        ],
        compiler_params=pltpu.CompilerParams(
            collective_id=0, has_side_effects=True, vmem_limit_bytes=48 * 1024 * 1024
        ),
        name="hyena_conv",
    )(*[pltpu.with_memory_space_constraint(x, pltpu.HBM) for x in operands])


def solution(mesh):
    placed = (
        P(("groups", "seq"), "chan"),
        P(("groups", "seq"), "chan"),
        P(("groups", "seq"), "chan"),
        P("seq", "chan"),
        P("chan"),
    )
    return jax.shard_map(
        functools.partial(shards, mesh.shape["seq"], mesh.shape["groups"]),
        mesh=mesh,
        in_specs=placed,
        out_specs=P(("groups", "seq"), "chan"),
        check_vma=False,
    )
```
